512 devices in a mesh: blk: 32 (over z_lo, y), seq: 16 (over z_hi, x, core).
Axes of the slice: x: 4, y: 4, z: 16 (z_hi: 2, z_lo: 8; z = z_hi * 8 + z_lo), core: 2. Of those that a mesh axis runs over, the one named last changes fastest.
Arguments:
- tokens: bfloat16 [12288, 4096], P('seq', 'blk'), may hold values from -6 to 6
- grad_out: bfloat16 [12288, 4096], P('seq', 'blk'), may hold values from -0.0546875 to 0.0546875
- input_weight_blocks: bfloat16 [1024, 128, 128], P('blk'), may hold values from -0.25 to 0.25
- output_weight_blocks: bfloat16 [1024, 128, 128], P('blk'), may hold values from -0.25 to 0.25
- row_ids: int32 [1024], P('blk'), may hold values from 0 to 31, as said below
- lengths: int32 [16], P('seq'), may hold values from 1 to 768, 7680 in all
Outputs:
- grad_in: bfloat16 [1024, 128, 128], P('blk', 'seq')
- grad_w_out: bfloat16 [1024, 128, 128], P('blk', 'seq')
The draws below stay inside these ranges and needn't reach their ends.
Inputs may be any that keep to these rules, and one draw needn't show every extreme that they name: `row_ids`: the 4 blocks of each hidden column block have distinct row blocks. `lengths`: some window is full.
All inputs are finite; a program needn't handle non-finite values. No bound on the sum of `lengths` on one device may be relied on, other than what follows from the above.
Results may differ from the reference program's by a relative error of at most 0.015.
Values may be sent and summed in bfloat16 or wider, within the bound.
No kernel may reach another device: no remote copies, remote signals or barrier semaphores. Data moves between devices by JAX's collectives and lax.ppermute only.
A program may use at most 64 MiB of HBM per device.

```python
import math
import jax
import jax.numpy as jnp
import numpy as np
from jax import lax

D = 4096
BLOCK_SIDE = 128
TP = 768
RB = 32
CB = 256
BLOCKS_PER_COLUMN = 4
SLOT_COUNT = 1024
TOKENS = 12288
N_SEQ = 16


def draw_row_ids(key, part):
    base_key = jax.random.fold_in(key, 11)
    row_order = jax.random.permutation(jax.random.fold_in(base_key, 1), RB)
    col_order = jax.random.permutation(jax.random.fold_in(base_key, 2), CB)
    offset_draw = jax.random.randint(jax.random.fold_in(base_key, 3), (), 0, RB)
    anchors = (col_order + offset_draw) % RB
    powers = jnp.left_shift(jnp.ones((BLOCKS_PER_COLUMN - 1,), jnp.int32), jnp.arange(BLOCKS_PER_COLUMN - 1, dtype=jnp.int32))
    offsets = jnp.concatenate([jnp.zeros((1,), jnp.int32), powers])
    picks = jnp.bitwise_xor(anchors[:, None].astype(jnp.int32), offsets[None, :])
    return row_order[picks].reshape(-1).astype(jnp.int32)


def level_of(own_key, shape, cuts, smallest, top_value):
    factor_of, own = 1.0, jax.random.fold_in(own_key, 6)
    for axis_at, blocks in cuts:
        heights = jnp.exp(jax.random.uniform(jax.random.fold_in(own, axis_at), (blocks,), jnp.float32, smallest / len(cuts), top_value / len(cuts)))
        factor_of = factor_of * jnp.repeat(heights, shape[axis_at] // blocks).reshape([-1 if axis == axis_at else 1 for axis in range(len(shape))])
    return factor_of


def split_up(number_of, total, bound, lean):
    weights = [(1 << 20) // math.isqrt(rank ** lean) + 1 for rank in range(2, number_of + 1)]
    surplus, holding = total - bound - (number_of - 1), [1] * (number_of - 1)
    while surplus > 0:
        movable = [i for i in range(number_of - 1) if holding[i] < bound]
        mass, remaining = sum([weights[i] for i in movable]), surplus
        for i in movable:
            extra = min(bound - holding[i], max(1, remaining * weights[i] // mass), surplus)
            holding[i] = holding[i] + extra
            surplus = surplus - extra
    return np.array([bound] + holding)


def ragged(stream_key, number_of, total, limit, slope):
    if number_of == 2:
        one = jax.random.randint(stream_key, (), max(1, total - limit), min(limit, total - 1) + 1)
        return jnp.stack([one, total - one])
    tallies = jnp.asarray(split_up(number_of, total, limit, slope), jnp.int32)
    pairs = (number_of - 1) // 2
    donor, receiver = tallies[1:1 + 2 * pairs:2], tallies[2:2 + 2 * pairs:2]
    slack = jnp.minimum(donor - 1, limit - receiver)
    passed = jax.random.randint(jax.random.fold_in(stream_key, 1), (pairs,), 0, 1 << 20) % (slack + 1)
    tallies = tallies.at[1:1 + 2 * pairs:2].set(donor - passed).at[2:2 + 2 * pairs:2].set(receiver + passed)
    return tallies[jax.random.permutation(jax.random.fold_in(stream_key, 2), number_of)]


def gaussian(stream_key, dims, spread, bound, shards=(), kind=jnp.bfloat16):
    values = jax.random.normal(stream_key, dims, jnp.float32) * spread
    if len(shards) > 0:
        values = level_of(stream_key, dims, shards, -0.22, 0.18) * values
    return jnp.clip(values, min=-bound, max=bound).astype(kind)


def setup_inputs(seed: int = 0) -> dict:
    splits = jax.random.split(jax.random.key(seed), 7)
    return {
        "tokens": gaussian(splits[0], (TOKENS, D), 1.0, 6.0, ((0, 16), (1, 32))),
        "grad_out": gaussian(splits[1], (TOKENS, D), TOKENS ** -0.5, 0.0546875, ((0, 16), (1, 32))),
        "input_weight_blocks": gaussian(splits[2], (SLOT_COUNT, BLOCK_SIDE, BLOCK_SIDE), (BLOCKS_PER_COLUMN * BLOCK_SIDE) ** -0.5, 0.25, ((0, 32),)),
        "output_weight_blocks": gaussian(splits[3], (SLOT_COUNT, BLOCK_SIDE, BLOCK_SIDE), (BLOCKS_PER_COLUMN * BLOCK_SIDE) ** -0.5, 0.25, ((0, 32),)),
        "row_ids": draw_row_ids(jax.random.fold_in(splits[6], 71), 0),
        "lengths": ragged(splits[5], N_SEQ, N_SEQ * TP * 5 // 8, TP, 2).astype(jnp.int32),
    }


gelu_scale = 0.7978845608


def gelu_pair(pre_act):
    tanh_val = jnp.tanh(gelu_scale * (pre_act + 0.044715 * pre_act * pre_act * pre_act))
    activation = 0.5 * pre_act * (1.0 + tanh_val)
    gelu_slope = 0.5 * (1.0 + tanh_val) + 0.5 * pre_act * (1.0 - tanh_val * tanh_val) * gelu_scale * (1.0 + 0.134145 * pre_act * pre_act)
    return activation, gelu_slope


def reference(tokens, grad_out, input_weight_blocks, output_weight_blocks, row_ids, lengths):
    live_rows = lax.iota(jnp.int32, TP)[None, :] < lengths[:, None]
    x_panels = tokens.reshape(N_SEQ, TP, RB, BLOCK_SIDE)
    g_panels = grad_out.reshape(N_SEQ, TP, RB, BLOCK_SIDE)
    masked = jnp.where(live_rows[:, :, None, None], g_panels, jnp.zeros_like(g_panels)).astype(jnp.bfloat16)
    w_in_f = input_weight_blocks.astype(jnp.float32)
    output_weight_flat = output_weight_blocks.astype(jnp.float32)

    def window_step(totals, panel_pair):
        x_panel, g_panel = panel_pair
        x_slots = x_panel[:, row_ids, :].astype(jnp.float32)
        gradient_slots = g_panel[:, row_ids, :].astype(jnp.float32)
        pre_slot = jnp.einsum("tkc,kch->tkh", x_slots, w_in_f)
        pre_act = pre_slot.reshape(TP, CB, BLOCKS_PER_COLUMN, BLOCK_SIDE).sum(2)
        activation, gelu_slope = gelu_pair(pre_act)
        activation = activation.astype(jnp.bfloat16)
        slot_gradient = jnp.einsum("xcn,cpn->xcp", gradient_slots, output_weight_flat)
        grad_act = slot_gradient.reshape(TP, CB, BLOCKS_PER_COLUMN, BLOCK_SIDE).sum(2)
        grad_pre = (grad_act * gelu_slope).astype(jnp.bfloat16)
        x_four = x_slots.reshape(TP, CB, BLOCKS_PER_COLUMN, BLOCK_SIDE)
        g_four = gradient_slots.reshape(TP, CB, BLOCKS_PER_COLUMN, BLOCK_SIDE)
        input_share = jnp.einsum("tgrc,tgh->grch", x_four, grad_pre.astype(jnp.float32))
        output_share = jnp.einsum("tgh,tgrf->grhf", activation.astype(jnp.float32), g_four)
        input_share = input_share.reshape(SLOT_COUNT, BLOCK_SIDE, BLOCK_SIDE).astype(jnp.bfloat16).astype(jnp.float32)
        output_share = output_share.reshape(SLOT_COUNT, BLOCK_SIDE, BLOCK_SIDE).astype(jnp.bfloat16).astype(jnp.float32)
        return (totals[0] + input_share, totals[1] + output_share), None

    empty_weight_block = jnp.zeros((SLOT_COUNT, BLOCK_SIDE, BLOCK_SIDE), jnp.float32)
    totals, unused = lax.scan(window_step, (empty_weight_block, empty_weight_block), (x_panels, masked))
    return totals[0].astype(jnp.bfloat16), totals[1].astype(jnp.bfloat16)
```

```python
import functools

import jax
import jax.numpy as jnp
from jax import lax
from jax.experimental import pallas as pl
from jax.experimental.pallas import tpu as pltpu
from jax.sharding import PartitionSpec as P

SIDE = 128
PER_COLUMN = 4
N_SEQ = 16
N_X = 4
N_Y = 4
N_Z = 8
N_DEAL = 8
LIVE = 7680
SIZES = (512, 576, 640, 768)
NOTE_ROWS = 8
CHUNKS = 4
DEAD = 256.0
RING = (0, 2, 4, 6, 7, 5, 3, 1)
PLACE = tuple(RING.index(z) for z in range(N_Z))
AXES = ("blk", "seq")
BATCHES = (((0, 1), 1), ((2, 7), 3), ((3, 4), 1), ((5, 6), 3))

gelu_scale = 0.7978845608


def gelu_pair(pre_act):
    tanh_val = jnp.tanh(gelu_scale * (pre_act + 0.044715 * pre_act * pre_act * pre_act))
    activation = 0.5 * pre_act * (1.0 + tanh_val)
    gelu_slope = 0.5 * (1.0 + tanh_val) + 0.5 * pre_act * (
        1.0 - tanh_val * tanh_val
    ) * gelu_scale * (1.0 + 0.134145 * pre_act * pre_act)
    return (activation, gelu_slope)


def move_z(value, step):
    pairs = [
        (z * N_Y + y, RING[(PLACE[z] + step) % N_Z] * N_Y + y)
        for z in range(N_Z)
        for y in range(N_Y)
    ]
    return lax.ppermute(value, "blk", pairs)


def swap_y(value, mask):
    pairs = [(z * N_Y + y, z * N_Y + (y ^ mask)) for z in range(N_Z) for y in range(N_Y)]
    return lax.ppermute(value, "blk", pairs)


def deal_kernel(length_ref, tokens_ref, grad_ref, out_ref):
    rows = tokens_ref.shape[0]
    out_rows = out_ref.shape[0]
    share, stride = rows // N_DEAL, out_rows // N_DEAL
    at = lax.broadcasted_iota(jnp.int32, (rows, SIDE), 0)
    marked = jnp.where(at < length_ref[0], tokens_ref[...].astype(jnp.float32), DEAD)
    both = jnp.concatenate([marked.astype(jnp.bfloat16), grad_ref[...]], axis=1)
    to = lax.broadcasted_iota(jnp.int32, (out_rows, rows), 0)
    source = lax.broadcasted_iota(jnp.int32, (out_rows, rows), 1)
    slot = source % N_DEAL * stride + source // N_DEAL
    pick = jnp.where(slot == to, 1.0, 0.0).astype(jnp.bfloat16)
    dealt = jnp.dot(pick, both, preferred_element_type=jnp.float32)
    place = place_in_share(out_rows, 2 * SIDE, stride)
    high = DEAD + 2.0 * (length_ref[0] // 32).astype(jnp.float32)
    low = DEAD + 2.0 * (length_ref[0] % 32).astype(jnp.float32)
    note = jnp.where(place == share, high, jnp.where(place == share + 1, low, DEAD))
    out_ref[...] = jnp.where(place < share, dealt, note).astype(jnp.bfloat16)


def place_in_share(rows, lanes, stride):
    row = lax.broadcasted_iota(jnp.int32, (rows, lanes), 0)
    start = jnp.zeros_like(row)
    for j in range(1, rows // stride):
        start = jnp.where(row >= j * stride, j * stride, start)
    return row - start


def pack_kernel(dealt_ref, out_ref, size_ref):
    rows, out_rows = dealt_ref.shape[0], out_ref.shape[0]
    share = out_rows // N_DEAL
    values = dealt_ref[:, :SIDE].astype(jnp.float32)
    live = jnp.broadcast_to(jnp.where(values[:, :1] < DEAD / 2, 1.0, 0.0), (rows, SIDE))
    place = place_in_share(rows, SIDE, rows // N_DEAL)
    weight = jnp.where(place == share, 16.0, jnp.where(place == share + 1, 0.5, 0.0))
    lane = lax.broadcasted_iota(jnp.int32, (rows, SIDE), 1)
    held = jnp.sum(jnp.where(lane == 0, weight * (values - DEAD), 0.0))
    most = jnp.maximum(held, LIVE - held).astype(jnp.int32) + (N_DEAL - 1) * N_DEAL
    size = jnp.int32(0)
    for smaller in SIZES[:-1]:
        size = size + (most > smaller * N_DEAL).astype(jnp.int32)
    size_ref[0] = size
    to = lax.broadcasted_iota(jnp.int32, (rows, rows), 0)
    source = lax.broadcasted_iota(jnp.int32, (rows, rows), 1)
    before = jnp.where(source < to, 1.0, 0.0).astype(jnp.bfloat16)
    rank = jnp.dot(before, live.astype(jnp.bfloat16), preferred_element_type=jnp.float32)
    rank = jnp.where(live > 0.5, rank, -1.0)[:, :1]
    slot = lax.broadcasted_iota(jnp.int32, (rows, out_rows), 1).astype(jnp.float32)
    pick = jnp.where(rank == slot, 1.0, 0.0).astype(jnp.bfloat16)
    out_ref[...] = lax.dot_general(
        pick, dealt_ref[...], (((0,), (0,)), ((), ())), preferred_element_type=jnp.float32
    ).astype(jnp.bfloat16)


def grad_kernel(slot_ref, core_ref, *refs):
    rows_at_once = refs[0].shape[0] // CHUNKS
    own = refs[:N_Z]
    passed = refs[N_Z : N_Z + 2 * len(BATCHES)]
    w_in_ref, w_out_ref, out_ref, held, hidden, summed, sems = refs[N_Z + 2 * len(BATCHES) :]
    copies = []

    def put(source, target):
        copies.append(pltpu.make_async_copy(source, target, sems.at[len(copies)]))

    for slot in range(N_Z):
        put(own[slot], held.at[slot * N_Y])
    for index, (batch, mask) in enumerate(BATCHES):
        near, far = passed[2 * index : 2 * index + 2]
        for i, slot in enumerate(batch):
            put(near.at[i], held.at[slot * N_Y + mask])
            put(far.at[i], held.at[slot * N_Y + (mask ^ 2)])
            put(far.at[i + len(batch)], held.at[slot * N_Y + 2])
    for copy in copies:
        copy.start()
    for copy in copies:
        copy.wait()
    core = core_ref[0]

    @pl.loop(0, w_in_ref.shape[0] // PER_COLUMN)
    def _(group):
        first = group * PER_COLUMN
        slots = [slot_ref[first + r] for r in range(PER_COLUMN)]
        w_in = jnp.concatenate([w_in_ref[first + r] for r in range(PER_COLUMN)], axis=0)
        w_out = jnp.concatenate([w_out_ref[first + r] for r in range(PER_COLUMN)], axis=1)

        @pl.loop(0, CHUNKS)
        def _(chunk):
            at = pl.ds(pl.multiple_of(chunk * rows_at_once, 16), rows_at_once)
            x = jnp.concatenate([held[s, at, :SIDE] for s in slots], axis=1)
            g = jnp.concatenate([held[s, at, SIDE:] for s in slots], axis=1)
            pre_act = jnp.dot(x, w_in, preferred_element_type=jnp.float32)
            activation, gelu_slope = gelu_pair(pre_act)
            grad_act = lax.dot_general(
                g, w_out, (((1,), (1,)), ((), ())), preferred_element_type=jnp.float32
            )
            hidden[0, at] = (grad_act * gelu_slope).astype(jnp.bfloat16)
            hidden[1, at] = activation.astype(jnp.bfloat16)

        x = jnp.concatenate([held[s, :, :SIDE] for s in slots], axis=1)
        g = jnp.concatenate([held[s, :, SIDE:] for s in slots], axis=1)
        over_rows = (((0,), (0,)), ((), ()))
        shares = (
            lax.dot_general(hidden[0], x, over_rows, preferred_element_type=jnp.float32),
            lax.dot_general(hidden[1], g, over_rows, preferred_element_type=jnp.float32),
        )
        for which, share in enumerate(shares):
            for r in range(PER_COLUMN):
                summed[which, r] = share[:, r * SIDE : (r + 1) * SIDE]

        @pl.loop(0, PER_COLUMN)
        def _(r):
            for which in range(2):
                block = summed[which, r]
                block = (block.T if which == 0 else block).astype(jnp.bfloat16)
                for seq in range(N_SEQ):
                    z_at, x_at, piece = seq // 8, seq % 8 // 2, seq % 2
                    out_ref[jnp.bitwise_xor(core, piece), x_at, z_at, which, first + r] = block[
                        seq * 8 : seq * 8 + 8
                    ]


def gather_and_differentiate(size, packed, slots, core, w_in, w_out):
    vmem = pl.BlockSpec(memory_space=pltpu.VMEM)
    smem = pl.BlockSpec(memory_space=pltpu.SMEM)
    any_space = pl.BlockSpec(memory_space=pl.ANY)
    n_slots = w_in.shape[0]
    blocks = {0: packed[:size]}
    for i in range(1, 5):
        blocks[i] = move_z(blocks[i - 1], 1)
        if i < 4:
            blocks[N_Z - i] = move_z(blocks[(N_Z - i + 1) % N_Z], -1)
    passed = []
    for batch, mask in BATCHES:
        value = jnp.stack([blocks[slot] for slot in batch])
        near = swap_y(value, mask)
        far = swap_y(jnp.concatenate([value, near]), mask ^ 2)
        passed += [near, far]
    return pl.pallas_call(
        grad_kernel,
        out_shape=jax.ShapeDtypeStruct((2, N_X, 2, 2, n_slots, 8, SIDE), jnp.bfloat16),
        in_specs=[smem, smem] + [any_space] * (N_Z + len(passed)) + [vmem, vmem],
        out_specs=vmem,
        scratch_shapes=[
            pltpu.VMEM((N_Y * N_Z, size, 2 * SIDE), jnp.bfloat16),
            pltpu.VMEM((2, size, SIDE), jnp.bfloat16),
            pltpu.VMEM((2, PER_COLUMN, SIDE, SIDE), jnp.float32),
            pltpu.SemaphoreType.DMA((N_Y * N_Z,)),
        ],
        name="weight_grads",
    )(slots, core, *[blocks[i] for i in range(N_Z)], *passed, w_in, w_out)


def shards(tokens, grad_out, input_weight_blocks, output_weight_blocks, row_ids, lengths):
    blk, seq = lax.axis_index("blk"), lax.axis_index("seq")
    rows = tokens.shape[0]
    vmem = pl.BlockSpec(memory_space=pltpu.VMEM)
    smem = pl.BlockSpec(memory_space=pltpu.SMEM)
    dealt = pl.pallas_call(
        deal_kernel,
        out_shape=jax.ShapeDtypeStruct((rows + N_DEAL * NOTE_ROWS, 2 * SIDE), jnp.bfloat16),
        in_specs=[smem, vmem, vmem],
        out_specs=vmem,
        name="deal",
    )(lengths, tokens, grad_out)
    halves = [[h * N_DEAL + i for i in range(N_DEAL)] for h in range(2)]
    dealt = lax.all_to_all(dealt, "seq", 0, 0, axis_index_groups=halves, tiled=True)
    packed, size = pl.pallas_call(
        pack_kernel,
        out_shape=(
            jax.ShapeDtypeStruct((rows, 2 * SIDE), jnp.bfloat16),
            jax.ShapeDtypeStruct((1,), jnp.int32),
        ),
        in_specs=[vmem],
        out_specs=(vmem, smem),
        name="pack",
    )(dealt)

    place = jnp.array(PLACE, jnp.int32)
    z_slot = (place[blk // N_Y] - place[row_ids // N_Y]) % N_Z
    slots = (z_slot * N_Y + jnp.bitwise_xor(blk, row_ids) % N_Y).astype(jnp.int32)
    shares = lax.switch(
        size[0],
        [functools.partial(gather_and_differentiate, n) for n in SIZES],
        packed,
        slots,
        (seq % 2).reshape(1),
        input_weight_blocks,
        output_weight_blocks,
    )

    swap = [(i, i ^ 1) for i in range(N_SEQ)]
    other = lax.ppermute(shares[1], "seq", swap)
    total = (shares[0].astype(jnp.float32) + other.astype(jnp.float32)).astype(jnp.bfloat16)
    along_x = [[h * 8 + x * 2 + c for x in range(N_X)] for h in range(2) for c in range(2)]
    total = lax.all_to_all(total, "seq", 0, 0, axis_index_groups=along_x, tiled=True)
    total = total.astype(jnp.float32).sum(0)
    mine = lax.dynamic_index_in_dim(total, seq // 8, 0, keepdims=False)
    theirs = lax.dynamic_index_in_dim(total, 1 - seq // 8, 0, keepdims=False)
    across = [(i, i ^ 8) for i in range(N_SEQ)]
    theirs = lax.ppermute(theirs.astype(jnp.bfloat16), "seq", across)
    total = (mine + theirs.astype(jnp.float32)).astype(jnp.bfloat16)
    return total[0], total[1]


def solution(mesh):
    return jax.shard_map(
        shards,
        mesh=mesh,
        in_specs=(
            P("seq", "blk"),
            P("seq", "blk"),
            P("blk", None, None),
            P("blk", None, None),
            P("blk"),
            P("seq"),
        ),
        out_specs=(P("blk", "seq", None), P("blk", "seq", None)),
        check_vma=False,
    )
```

```python
import functools

import jax
import jax.numpy as jnp
from jax import lax
from jax.experimental import pallas as pl
from jax.experimental.pallas import tpu as pltpu
from jax.sharding import PartitionSpec as P

SIDE = 128
PER_COLUMN = 4
N_SEQ = 16
N_X = 4
N_Y = 4
N_Z = 8
N_DEAL = 8
LIVE = 7680
SIZES = (512, 576, 640, 768)
NOTE_ROWS = 8
DEAD = 256.0
RING = (0, 2, 4, 6, 7, 5, 3, 1)
PLACE = tuple(RING.index(z) for z in range(N_Z))
AXES = ("blk", "seq")
BATCHES = (((0, 1), 1), ((2, 7), 3), ((3, 4), 1), ((5, 6), 3))

gelu_scale = 0.7978845608


def gelu_pair(pre_act):
    tanh_val = jnp.tanh(gelu_scale * (pre_act + 0.044715 * pre_act * pre_act * pre_act))
    activation = 0.5 * pre_act * (1.0 + tanh_val)
    gelu_slope = 0.5 * (1.0 + tanh_val) + 0.5 * pre_act * (
        1.0 - tanh_val * tanh_val
    ) * gelu_scale * (1.0 + 0.134145 * pre_act * pre_act)
    return (activation, gelu_slope)


def move_z(value, step):
    pairs = [
        (z * N_Y + y, RING[(PLACE[z] + step) % N_Z] * N_Y + y)
        for z in range(N_Z)
        for y in range(N_Y)
    ]
    return lax.ppermute(value, "blk", pairs)


def swap_y(value, mask):
    pairs = [(z * N_Y + y, z * N_Y + (y ^ mask)) for z in range(N_Z) for y in range(N_Y)]
    return lax.ppermute(value, "blk", pairs)


def deal_kernel(length_ref, tokens_ref, grad_ref, out_ref):
    rows = tokens_ref.shape[0]
    out_rows = out_ref.shape[0]
    share, stride = rows // N_DEAL, out_rows // N_DEAL
    at = lax.broadcasted_iota(jnp.int32, (rows, SIDE), 0)
    marked = jnp.where(at < length_ref[0], tokens_ref[...].astype(jnp.float32), DEAD)
    both = jnp.concatenate([marked.astype(jnp.bfloat16), grad_ref[...]], axis=1)
    to = lax.broadcasted_iota(jnp.int32, (out_rows, rows), 0)
    source = lax.broadcasted_iota(jnp.int32, (out_rows, rows), 1)
    slot = source % N_DEAL * stride + source // N_DEAL
    pick = jnp.where(slot == to, 1.0, 0.0).astype(jnp.bfloat16)
    dealt = jnp.dot(pick, both, preferred_element_type=jnp.float32)
    place = place_in_share(out_rows, 2 * SIDE, stride)
    high = DEAD + 2.0 * (length_ref[0] // 32).astype(jnp.float32)
    low = DEAD + 2.0 * (length_ref[0] % 32).astype(jnp.float32)
    note = jnp.where(place == share, high, jnp.where(place == share + 1, low, DEAD))
    out_ref[...] = jnp.where(place < share, dealt, note).astype(jnp.bfloat16)


def place_in_share(rows, lanes, stride):
    row = lax.broadcasted_iota(jnp.int32, (rows, lanes), 0)
    start = jnp.zeros_like(row)
    for j in range(1, rows // stride):
        start = jnp.where(row >= j * stride, j * stride, start)
    return row - start


def pack_kernel(dealt_ref, out_ref, size_ref):
    rows, out_rows = dealt_ref.shape[0], out_ref.shape[0]
    share = out_rows // N_DEAL
    values = dealt_ref[:, :SIDE].astype(jnp.float32)
    live = jnp.broadcast_to(jnp.where(values[:, :1] < DEAD / 2, 1.0, 0.0), (rows, SIDE))
    place = place_in_share(rows, SIDE, rows // N_DEAL)
    weight = jnp.where(place == share, 16.0, jnp.where(place == share + 1, 0.5, 0.0))
    lane = lax.broadcasted_iota(jnp.int32, (rows, SIDE), 1)
    held = jnp.sum(jnp.where(lane == 0, weight * (values - DEAD), 0.0))
    most = jnp.maximum(held, LIVE - held).astype(jnp.int32) + (N_DEAL - 1) * N_DEAL
    size = jnp.int32(0)
    for smaller in SIZES[:-1]:
        size = size + (most > smaller * N_DEAL).astype(jnp.int32)
    size_ref[0] = size
    to = lax.broadcasted_iota(jnp.int32, (rows, rows), 0)
    source = lax.broadcasted_iota(jnp.int32, (rows, rows), 1)
    before = jnp.where(source < to, 1.0, 0.0).astype(jnp.bfloat16)
    rank = jnp.dot(before, live.astype(jnp.bfloat16), preferred_element_type=jnp.float32)
    rank = jnp.where(live > 0.5, rank, -1.0)[:, :1]
    slot = lax.broadcasted_iota(jnp.int32, (rows, out_rows), 1).astype(jnp.float32)
    pick = jnp.where(rank == slot, 1.0, 0.0).astype(jnp.bfloat16)
    out_ref[...] = lax.dot_general(
        pick, dealt_ref[...], (((0,), (0,)), ((), ())), preferred_element_type=jnp.float32
    ).astype(jnp.bfloat16)


def whereabouts():
    found = [0] * (N_Z * N_Y)
    for slot in range(N_Z):
        found[slot * N_Y] = 4 * slot
    for index, (batch, mask) in enumerate(BATCHES):
        near = 4 * (N_Z + 2 * index)
        for i, slot in enumerate(batch):
            found[slot * N_Y + mask] = near + i
            found[slot * N_Y + (mask ^ 2)] = near + 4 + i
            found[slot * N_Y + 2] = near + 4 + len(batch) + i
    return found


def grad_kernel(where_ref, *refs):
    n_held = N_Z + 2 * len(BATCHES)
    held = refs[:n_held]
    w_in_ref, w_out_ref, even, odd, four, sems = refs[n_held:]
    groups = even.shape[3] // PER_COLUMN

    def fetch(group, into):
        for r in range(PER_COLUMN):
            where = where_ref[group * PER_COLUMN + r]
            for i, ref in enumerate(held):

                def start(ref=ref, r=r, where=where):
                    block = ref if len(ref.shape) == 2 else ref.at[where % 4]
                    pltpu.make_async_copy(block, four.at[into, r], sems.at[into, r]).start()

                pl.when(where // 4 == i)(start)

    fetch(0, 0)

    @pl.loop(0, groups)
    def _(group):
        now = group % 2

        @pl.when(group + 1 < groups)
        def _():
            fetch(group + 1, 1 - now)

        for r in range(PER_COLUMN):
            pltpu.make_async_copy(held[0], four.at[now, r], sems.at[now, r]).wait()
        first = group * PER_COLUMN
        x = jnp.concatenate([four[now, r, :, :SIDE] for r in range(PER_COLUMN)], axis=1)
        g = jnp.concatenate([four[now, r, :, SIDE:] for r in range(PER_COLUMN)], axis=1)
        w_in = jnp.concatenate([w_in_ref[first + r] for r in range(PER_COLUMN)], axis=0)
        w_out = jnp.concatenate([w_out_ref[first + r] for r in range(PER_COLUMN)], axis=1)
        pre_act = jnp.dot(x, w_in, preferred_element_type=jnp.float32)
        activation, gelu_slope = gelu_pair(pre_act)
        grad_act = lax.dot_general(
            g, w_out, (((1,), (1,)), ((), ())), preferred_element_type=jnp.float32
        )
        grad_pre = (grad_act * gelu_slope).astype(jnp.bfloat16)
        over_rows = (((0,), (0,)), ((), ()))
        shares = (
            lax.dot_general(grad_pre, x, over_rows, preferred_element_type=jnp.float32),
            lax.dot_general(
                activation.astype(jnp.bfloat16), g, over_rows, preferred_element_type=jnp.float32
            ),
        )
        for which, share in enumerate(shares):
            for r in range(PER_COLUMN):
                block = share[:, r * SIDE : (r + 1) * SIDE]
                block = (block.T if which == 0 else block).astype(jnp.bfloat16)
                for seq in range(N_SEQ):
                    target = odd if seq % 2 else even
                    target[seq % 8 // 2, seq // 8, which, first + r] = block[
                        seq * 8 : seq * 8 + 8
                    ]


def add_cores(even, odd, seq):
    swap = [(i, i ^ 1) for i in range(N_SEQ)]
    at_odd = seq % 2 == 1
    theirs = lax.ppermute(jnp.where(at_odd, even, odd), "seq", swap)
    mine = jnp.where(at_odd, odd, even)
    return (mine.astype(jnp.float32) + theirs.astype(jnp.float32)).astype(jnp.bfloat16)


def add_along_x(total):
    along_x = [[h * 8 + x * 2 + c for x in range(N_X)] for h in range(2) for c in range(2)]
    total = lax.all_to_all(total, "seq", 0, 0, axis_index_groups=along_x, tiled=True)
    return total.astype(jnp.float32).sum(0)


def add_halves(total, seq):
    across = [(i, i ^ 8) for i in range(N_SEQ)]
    at_high = seq >= N_DEAL
    theirs = jnp.where(at_high, total[0], total[1]).astype(jnp.bfloat16)
    theirs = lax.ppermute(theirs, "seq", across)
    return (jnp.where(at_high, total[1], total[0]) + theirs.astype(jnp.float32)).astype(jnp.bfloat16)


def gather_and_differentiate(size, packed, slots, w_in, w_out):
    vmem = pl.BlockSpec(memory_space=pltpu.VMEM)
    smem = pl.BlockSpec(memory_space=pltpu.SMEM)
    n_slots = w_in.shape[0]
    blocks = {0: packed[:size]}
    for i in range(1, 5):
        blocks[i] = move_z(blocks[i - 1], 1)
        if i < 4:
            blocks[N_Z - i] = move_z(blocks[(N_Z - i + 1) % N_Z], -1)
    passed = []
    for batch, mask in BATCHES:
        value = jnp.stack([blocks[slot] for slot in batch])
        near = swap_y(value, mask)
        far = swap_y(jnp.concatenate([value, near]), mask ^ 2)
        passed += [near, far]
    any_space = pl.BlockSpec(memory_space=pl.ANY)
    piece = jax.ShapeDtypeStruct((N_X, 2, 2, n_slots, 8, SIDE), jnp.bfloat16)
    return pl.pallas_call(
        grad_kernel,
        out_shape=[piece] * 2,
        in_specs=[smem] + [any_space] * (N_Z + len(passed)) + [vmem] * 2,
        out_specs=[vmem] * 2,
        scratch_shapes=[
            pltpu.VMEM((2, PER_COLUMN, size, 2 * SIDE), jnp.bfloat16),
            pltpu.SemaphoreType.DMA((2, PER_COLUMN)),
        ],
        name="weight_grads",
    )(slots, *[blocks[i] for i in range(N_Z)], *passed, w_in, w_out)


def shards(tokens, grad_out, input_weight_blocks, output_weight_blocks, row_ids, lengths):
    blk, seq = lax.axis_index("blk"), lax.axis_index("seq")
    rows = tokens.shape[0]
    vmem = pl.BlockSpec(memory_space=pltpu.VMEM)
    smem = pl.BlockSpec(memory_space=pltpu.SMEM)
    dealt = pl.pallas_call(
        deal_kernel,
        out_shape=jax.ShapeDtypeStruct((rows + N_DEAL * NOTE_ROWS, 2 * SIDE), jnp.bfloat16),
        in_specs=[smem, vmem, vmem],
        out_specs=vmem,
        name="deal",
    )(lengths, tokens, grad_out)
    halves = [[h * N_DEAL + i for i in range(N_DEAL)] for h in range(2)]
    dealt = lax.all_to_all(dealt, "seq", 0, 0, axis_index_groups=halves, tiled=True)
    packed, size = pl.pallas_call(
        pack_kernel,
        out_shape=(
            jax.ShapeDtypeStruct((rows, 2 * SIDE), jnp.bfloat16),
            jax.ShapeDtypeStruct((1,), jnp.int32),
        ),
        in_specs=[vmem],
        out_specs=(vmem, smem),
        name="pack",
    )(dealt)

    place = jnp.array(PLACE, jnp.int32)
    z_slot = (place[blk // N_Y] - place[row_ids // N_Y]) % N_Z
    slots = (z_slot * N_Y + jnp.bitwise_xor(blk, row_ids) % N_Y).astype(jnp.int32)
    slots = jnp.array(whereabouts(), jnp.int32)[slots]
    even, odd = lax.switch(
        size[0],
        [functools.partial(gather_and_differentiate, n) for n in SIZES],
        packed,
        slots,
        input_weight_blocks,
        output_weight_blocks,
    )
    total = add_halves(add_along_x(add_cores(even, odd, seq)), seq)
    return total[0], total[1]


def solution(mesh):
    return jax.shard_map(
        shards,
        mesh=mesh,
        in_specs=(
            P("seq", "blk"),
            P("seq", "blk"),
            P("blk", None, None),
            P("blk", None, None),
            P("blk"),
            P("seq"),
        ),
        out_specs=(P("blk", "seq", None), P("blk", "seq", None)),
        check_vma=False,
    )
```

```python
import functools

import jax
import jax.numpy as jnp
from jax import lax
from jax.experimental import pallas as pl
from jax.experimental.pallas import tpu as pltpu
from jax.sharding import PartitionSpec as P

SIDE = 128
PER_COLUMN = 4
N_SEQ = 16
N_X = 4
N_Y = 4
N_Z = 8
N_DEAL = 8
LIVE = 7680
SIZES = (512, 544, 576, 624, 768)
NOTE_ROWS = 8
DEAD = 256.0
RING = (0, 2, 4, 6, 7, 5, 3, 1)
PLACE = tuple(RING.index(z) for z in range(N_Z))
BATCHES = (((0, 1), 1), ((2, 7), 3), ((3, 4), 1), ((5, 6), 3))

gelu_scale = 0.7978845608


def gelu_pair(pre_act):
    tanh_val = jnp.tanh(gelu_scale * (pre_act + 0.044715 * pre_act * pre_act * pre_act))
    activation = 0.5 * pre_act * (1.0 + tanh_val)
    gelu_slope = 0.5 * (1.0 + tanh_val) + 0.5 * pre_act * (
        1.0 - tanh_val * tanh_val
    ) * gelu_scale * (1.0 + 0.134145 * pre_act * pre_act)
    return (activation, gelu_slope)


def move_z(value, step):
    pairs = [
        (z * N_Y + y, RING[(PLACE[z] + step) % N_Z] * N_Y + y)
        for z in range(N_Z)
        for y in range(N_Y)
    ]
    return lax.ppermute(value, "blk", pairs)


def swap_y(value, mask):
    pairs = [(z * N_Y + y, z * N_Y + (y ^ mask)) for z in range(N_Z) for y in range(N_Y)]
    return lax.ppermute(value, "blk", pairs)


def deal_kernel(length_ref, tokens_ref, grad_ref, out_ref):
    rows = tokens_ref.shape[0]
    out_rows = out_ref.shape[0]
    share, stride = rows // N_DEAL, out_rows // N_DEAL
    at = lax.broadcasted_iota(jnp.int32, (rows, SIDE), 0)
    marked = jnp.where(at < length_ref[0], tokens_ref[...].astype(jnp.float32), DEAD)
    both = jnp.concatenate([marked.astype(jnp.bfloat16), grad_ref[...]], axis=1)
    to = lax.broadcasted_iota(jnp.int32, (out_rows, rows), 0)
    source = lax.broadcasted_iota(jnp.int32, (out_rows, rows), 1)
    slot = source % N_DEAL * stride + source // N_DEAL
    pick = jnp.where(slot == to, 1.0, 0.0).astype(jnp.bfloat16)
    dealt = jnp.dot(pick, both, preferred_element_type=jnp.float32)
    place = place_in_share(out_rows, 2 * SIDE, stride)
    high = DEAD + 2.0 * (length_ref[0] // 32).astype(jnp.float32)
    low = DEAD + 2.0 * (length_ref[0] % 32).astype(jnp.float32)
    note = jnp.where(place == share, high, jnp.where(place == share + 1, low, DEAD))
    out_ref[...] = jnp.where(place < share, dealt, note).astype(jnp.bfloat16)


def place_in_share(rows, lanes, stride):
    row = lax.broadcasted_iota(jnp.int32, (rows, lanes), 0)
    start = jnp.zeros_like(row)
    for j in range(1, rows // stride):
        start = jnp.where(row >= j * stride, j * stride, start)
    return row - start


def pack_kernel(dealt_ref, out_ref, size_ref):
    rows, out_rows = dealt_ref.shape[0], out_ref.shape[0]
    share = out_rows // N_DEAL
    values = dealt_ref[:, :SIDE].astype(jnp.float32)
    live = jnp.broadcast_to(jnp.where(values[:, :1] < DEAD / 2, 1.0, 0.0), (rows, SIDE))
    place = place_in_share(rows, SIDE, rows // N_DEAL)
    weight = jnp.where(place == share, 16.0, jnp.where(place == share + 1, 0.5, 0.0))
    lane = lax.broadcasted_iota(jnp.int32, (rows, SIDE), 1)
    held = jnp.sum(jnp.where(lane == 0, weight * (values - DEAD), 0.0))
    most = jnp.maximum(held, LIVE - held).astype(jnp.int32) + (N_DEAL - 1) * N_DEAL
    size = jnp.int32(0)
    for smaller in SIZES[:-1]:
        size = size + (most > smaller * N_DEAL).astype(jnp.int32)
    size_ref[0] = size
    stride, ahead, ranks = rows // N_DEAL, jnp.zeros((1, SIDE), jnp.float32), []
    for j in range(N_DEAL):
        here = live[j * stride : (j + 1) * stride]
        at = lax.broadcasted_iota(jnp.int32, (stride, SIDE), 0).astype(jnp.float32)
        ranks.append(jnp.where(here > 0.5, at + ahead, -1.0))
        ahead = ahead + jnp.sum(here, axis=0, keepdims=True)
    rank = jnp.concatenate(ranks, axis=0)[:, :1]
    slot = lax.broadcasted_iota(jnp.int32, (rows, out_rows), 1).astype(jnp.float32)
    pick = jnp.where(rank == slot, 1.0, 0.0).astype(jnp.bfloat16)
    out_ref[...] = lax.dot_general(
        pick, dealt_ref[...], (((0,), (0,)), ((), ())), preferred_element_type=jnp.float32
    ).astype(jnp.bfloat16)


def whereabouts():
    found = [0] * (N_Z * N_Y)
    for slot in range(N_Z):
        found[slot * N_Y] = 4 * slot
    for index, (batch, mask) in enumerate(BATCHES):
        near = 4 * (N_Z + 2 * index)
        for i, slot in enumerate(batch):
            found[slot * N_Y + mask] = near + i
            found[slot * N_Y + (mask ^ 2)] = near + 4 + i
            found[slot * N_Y + 2] = near + 4 + len(batch) + i
    return found


def grad_kernel(where_ref, *refs):
    n_held = N_Z + 2 * len(BATCHES)
    held = refs[:n_held]
    w_in_ref, w_out_ref, even, odd, four, sems = refs[n_held:]
    groups = even.shape[3] // PER_COLUMN

    def fetch(group, into):
        for r in range(PER_COLUMN):
            where = where_ref[group * PER_COLUMN + r]
            for i, ref in enumerate(held):

                def start(ref=ref, r=r, where=where):
                    block = ref if len(ref.shape) == 2 else ref.at[where % 4]
                    pltpu.make_async_copy(block, four.at[into, r], sems.at[into, r]).start()

                pl.when(where // 4 == i)(start)

    fetch(0, 0)

    @pl.loop(0, groups)
    def _(group):
        now = group % 2

        @pl.when(group + 1 < groups)
        def _():
            fetch(group + 1, 1 - now)

        for r in range(PER_COLUMN):
            pltpu.make_async_copy(held[0], four.at[now, r], sems.at[now, r]).wait()
        first = group * PER_COLUMN
        x = jnp.concatenate([four[now, r, :, :SIDE] for r in range(PER_COLUMN)], axis=1)
        g = jnp.concatenate([four[now, r, :, SIDE:] for r in range(PER_COLUMN)], axis=1)
        w_in = jnp.concatenate([w_in_ref[first + r] for r in range(PER_COLUMN)], axis=0)
        w_out = jnp.concatenate([w_out_ref[first + r] for r in range(PER_COLUMN)], axis=1)
        pre_act = jnp.dot(x, w_in, preferred_element_type=jnp.float32)
        activation, gelu_slope = gelu_pair(pre_act)
        grad_act = lax.dot_general(
            g, w_out, (((1,), (1,)), ((), ())), preferred_element_type=jnp.float32
        )
        grad_pre = (grad_act * gelu_slope).astype(jnp.bfloat16)
        over_rows = (((0,), (0,)), ((), ()))
        shares = (
            lax.dot_general(grad_pre, x, over_rows, preferred_element_type=jnp.float32),
            lax.dot_general(
                activation.astype(jnp.bfloat16), g, over_rows, preferred_element_type=jnp.float32
            ),
        )
        for which, share in enumerate(shares):
            for r in range(PER_COLUMN):
                block = share[:, r * SIDE : (r + 1) * SIDE]
                block = (block.T if which == 0 else block).astype(jnp.bfloat16)
                for seq in range(N_SEQ):
                    target = odd if seq % 2 else even
                    target[seq % 8 // 2, seq // 8, which, first + r] = block[
                        seq * 8 : seq * 8 + 8
                    ]


def add_cores(even, odd, seq):
    swap = [(i, i ^ 1) for i in range(N_SEQ)]
    at_odd = seq % 2 == 1
    theirs = lax.ppermute(jnp.where(at_odd, even, odd), "seq", swap)
    mine = jnp.where(at_odd, odd, even)
    return (mine.astype(jnp.float32) + theirs.astype(jnp.float32)).astype(jnp.bfloat16)


def add_along_x(total):
    along_x = [[h * 8 + x * 2 + c for x in range(N_X)] for h in range(2) for c in range(2)]
    total = lax.all_to_all(total, "seq", 0, 0, axis_index_groups=along_x, tiled=True)
    return total.astype(jnp.float32).sum(0)


def add_halves(total, seq):
    across = [(i, i ^ 8) for i in range(N_SEQ)]
    at_high = seq >= N_DEAL
    theirs = jnp.where(at_high, total[0], total[1]).astype(jnp.bfloat16)
    theirs = lax.ppermute(theirs, "seq", across)
    return (jnp.where(at_high, total[1], total[0]) + theirs.astype(jnp.float32)).astype(jnp.bfloat16)


def gather_and_differentiate(size, packed, slots, w_in, w_out):
    vmem = pl.BlockSpec(memory_space=pltpu.VMEM)
    smem = pl.BlockSpec(memory_space=pltpu.SMEM)
    n_slots = w_in.shape[0]
    blocks = {0: packed[:size]}
    passed = []

    def start_along_y(index):
        batch, mask = BATCHES[index]
        value = jnp.stack([blocks[slot] for slot in batch])
        passed.append((value, swap_y(value, mask)))
        return passed[-1][1]

    for i in range(1, 5):
        ahead, behind = blocks[i - 1], blocks[(N_Z - i + 1) % N_Z]
        if i > 2:
            ahead, behind, _ = lax.optimization_barrier((ahead, behind, start_along_y(i - 3)))
        blocks[i] = move_z(ahead, 1)
        if i < 4:
            blocks[N_Z - i] = move_z(behind, -1)
    for index in range(len(passed), len(BATCHES)):
        start_along_y(index)
    passed = [
        part
        for (value, near), (_, mask) in zip(passed, BATCHES)
        for part in (near, swap_y(jnp.concatenate([value, near]), mask ^ 2))
    ]
    any_space = pl.BlockSpec(memory_space=pl.ANY)
    piece = jax.ShapeDtypeStruct((N_X, 2, 2, n_slots, 8, SIDE), jnp.bfloat16)
    return pl.pallas_call(
        grad_kernel,
        out_shape=[piece] * 2,
        in_specs=[smem] + [any_space] * (N_Z + len(passed)) + [vmem] * 2,
        out_specs=[vmem] * 2,
        scratch_shapes=[
            pltpu.VMEM((2, PER_COLUMN, size, 2 * SIDE), jnp.bfloat16),
            pltpu.SemaphoreType.DMA((2, PER_COLUMN)),
        ],
        name="weight_grads",
    )(slots, *[blocks[i] for i in range(N_Z)], *passed, w_in, w_out)


def shards(tokens, grad_out, input_weight_blocks, output_weight_blocks, row_ids, lengths):
    blk, seq = lax.axis_index("blk"), lax.axis_index("seq")
    rows = tokens.shape[0]
    vmem = pl.BlockSpec(memory_space=pltpu.VMEM)
    smem = pl.BlockSpec(memory_space=pltpu.SMEM)
    dealt = pl.pallas_call(
        deal_kernel,
        out_shape=jax.ShapeDtypeStruct((rows + N_DEAL * NOTE_ROWS, 2 * SIDE), jnp.bfloat16),
        in_specs=[smem, vmem, vmem],
        out_specs=vmem,
        name="deal",
    )(lengths, tokens, grad_out)
    halves = [[h * N_DEAL + i for i in range(N_DEAL)] for h in range(2)]
    dealt = lax.all_to_all(dealt, "seq", 0, 0, axis_index_groups=halves, tiled=True)
    packed, size = pl.pallas_call(
        pack_kernel,
        out_shape=(
            jax.ShapeDtypeStruct((rows, 2 * SIDE), jnp.bfloat16),
            jax.ShapeDtypeStruct((1,), jnp.int32),
        ),
        in_specs=[vmem],
        out_specs=(vmem, smem),
        name="pack",
    )(dealt)

    place = jnp.array(PLACE, jnp.int32)
    z_slot = (place[blk // N_Y] - place[row_ids // N_Y]) % N_Z
    slots = (z_slot * N_Y + jnp.bitwise_xor(blk, row_ids) % N_Y).astype(jnp.int32)
    slots = jnp.array(whereabouts(), jnp.int32)[slots]
    even, odd = lax.switch(
        size[0],
        [functools.partial(gather_and_differentiate, n) for n in SIZES],
        packed,
        slots,
        input_weight_blocks,
        output_weight_blocks,
    )
    total = add_halves(add_along_x(add_cores(even, odd, seq)), seq)
    return total[0], total[1]


def solution(mesh):
    return jax.shard_map(
        shards,
        mesh=mesh,
        in_specs=(
            P("seq", "blk"),
            P("seq", "blk"),
            P("blk", None, None),
            P("blk", None, None),
            P("blk"),
            P("seq"),
        ),
        out_specs=(P("blk", "seq", None), P("blk", "seq", None)),
        check_vma=False,
    )
```

```python
import functools

import jax
import jax.numpy as jnp
from jax import lax
from jax.experimental import pallas as pl
from jax.experimental.pallas import tpu as pltpu
from jax.sharding import PartitionSpec as P

SIDE = 128
PER_COLUMN = 4
N_SEQ = 16
N_X = 4
N_Y = 4
N_Z = 8
N_DEAL = 8
LIVE = 7680
SIZES = (512, 544, 576, 624, 768)
NOTE_ROWS = 8
DEAD = 256.0
RING = (0, 2, 4, 6, 7, 5, 3, 1)
PLACE = tuple(RING.index(z) for z in range(N_Z))
BATCHES = (((0, 1), 1), ((2, 7), 3), ((3, 4), 1), ((5, 6), 3))

gelu_scale = 0.7978845608


def gelu_pair(pre_act):
    tanh_val = jnp.tanh(gelu_scale * (pre_act + 0.044715 * pre_act * pre_act * pre_act))
    activation = 0.5 * pre_act * (1.0 + tanh_val)
    gelu_slope = 0.5 * (1.0 + tanh_val) + 0.5 * pre_act * (
        1.0 - tanh_val * tanh_val
    ) * gelu_scale * (1.0 + 0.134145 * pre_act * pre_act)
    return (activation, gelu_slope)


def move_z(value, step):
    pairs = [
        (z * N_Y + y, RING[(PLACE[z] + step) % N_Z] * N_Y + y)
        for z in range(N_Z)
        for y in range(N_Y)
    ]
    return lax.ppermute(value, "blk", pairs)


def swap_y(value, mask):
    pairs = [(z * N_Y + y, z * N_Y + (y ^ mask)) for z in range(N_Z) for y in range(N_Y)]
    return lax.ppermute(value, "blk", pairs)


def deal_kernel(length_ref, flip_ref, tokens_ref, grad_ref, out_ref):
    rows = tokens_ref.shape[0]
    out_rows = out_ref.shape[0]
    share, stride = rows // N_DEAL, out_rows // N_DEAL
    at = lax.broadcasted_iota(jnp.int32, (rows, SIDE), 0)
    marked = jnp.where(at < length_ref[0], tokens_ref[...].astype(jnp.float32), DEAD)
    both = jnp.concatenate([marked.astype(jnp.bfloat16), grad_ref[...]], axis=1)
    to = lax.broadcasted_iota(jnp.int32, (out_rows, rows), 0)
    source = lax.broadcasted_iota(jnp.int32, (out_rows, rows), 1)
    slot = jnp.bitwise_xor(source % N_DEAL, flip_ref[0]) * stride + source // N_DEAL
    pick = jnp.where(slot == to, 1.0, 0.0).astype(jnp.bfloat16)
    dealt = jnp.dot(pick, both, preferred_element_type=jnp.float32)
    place = place_in_share(out_rows, 2 * SIDE, stride)
    high = DEAD + 2.0 * (length_ref[0] // 32).astype(jnp.float32)
    low = DEAD + 2.0 * (length_ref[0] % 32).astype(jnp.float32)
    note = jnp.where(place == share, high, jnp.where(place == share + 1, low, DEAD))
    out_ref[...] = jnp.where(place < share, dealt, note).astype(jnp.bfloat16)


def place_in_share(rows, lanes, stride):
    row = lax.broadcasted_iota(jnp.int32, (rows, lanes), 0)
    start = jnp.zeros_like(row)
    for j in range(1, rows // stride):
        start = jnp.where(row >= j * stride, j * stride, start)
    return row - start


def pack_kernel(dealt_ref, out_ref, size_ref):
    rows, out_rows = dealt_ref.shape[0], out_ref.shape[0]
    share = out_rows // N_DEAL
    values = dealt_ref[:, :SIDE].astype(jnp.float32)
    live = jnp.broadcast_to(jnp.where(values[:, :1] < DEAD / 2, 1.0, 0.0), (rows, SIDE))
    place = place_in_share(rows, SIDE, rows // N_DEAL)
    weight = jnp.where(place == share, 16.0, jnp.where(place == share + 1, 0.5, 0.0))
    lane = lax.broadcasted_iota(jnp.int32, (rows, SIDE), 1)
    held = jnp.sum(jnp.where(lane == 0, weight * (values - DEAD), 0.0))
    most = jnp.maximum(held, LIVE - held).astype(jnp.int32) + (N_DEAL - 1) * N_DEAL // 2
    size = jnp.int32(0)
    for smaller in SIZES[:-1]:
        size = size + (most > smaller * N_DEAL).astype(jnp.int32)
    size_ref[0] = size
    stride, ahead, ranks = rows // N_DEAL, jnp.zeros((1, SIDE), jnp.float32), []
    for j in range(N_DEAL):
        here = live[j * stride : (j + 1) * stride]
        at = lax.broadcasted_iota(jnp.int32, (stride, SIDE), 0).astype(jnp.float32)
        ranks.append(jnp.where(here > 0.5, at + ahead, -1.0))
        ahead = ahead + jnp.sum(here, axis=0, keepdims=True)
    rank = jnp.concatenate(ranks, axis=0)[:, :1]
    slot = lax.broadcasted_iota(jnp.int32, (rows, out_rows), 1).astype(jnp.float32)
    pick = jnp.where(rank == slot, 1.0, 0.0).astype(jnp.bfloat16)
    out_ref[...] = lax.dot_general(
        pick, dealt_ref[...], (((0,), (0,)), ((), ())), preferred_element_type=jnp.float32
    ).astype(jnp.bfloat16)


def whereabouts():
    found = [0] * (N_Z * N_Y)
    for slot in range(N_Z):
        found[slot * N_Y] = 4 * slot
    for index, (batch, mask) in enumerate(BATCHES):
        near = 4 * (N_Z + 2 * index)
        for i, slot in enumerate(batch):
            found[slot * N_Y + mask] = near + i
            found[slot * N_Y + (mask ^ 2)] = near + 4 + i
            found[slot * N_Y + 2] = near + 4 + len(batch) + i
    return found


def grad_kernel(where_ref, *refs):
    n_held = N_Z + 2 * len(BATCHES)
    held = refs[:n_held]
    w_in_ref, w_out_ref, even, odd, four, sems = refs[n_held:]
    groups = even.shape[3] // PER_COLUMN

    def fetch(group, into):
        for r in range(PER_COLUMN):
            where = where_ref[group * PER_COLUMN + r]
            for i, ref in enumerate(held):

                def start(ref=ref, r=r, where=where):
                    block = ref if len(ref.shape) == 2 else ref.at[where % 4]
                    pltpu.make_async_copy(block, four.at[into, r], sems.at[into, r]).start()

                pl.when(where // 4 == i)(start)

    fetch(0, 0)

    @pl.loop(0, groups)
    def _(group):
        now = group % 2

        @pl.when(group + 1 < groups)
        def _():
            fetch(group + 1, 1 - now)

        for r in range(PER_COLUMN):
            pltpu.make_async_copy(held[0], four.at[now, r], sems.at[now, r]).wait()
        first = group * PER_COLUMN
        x = jnp.concatenate([four[now, r, :, :SIDE] for r in range(PER_COLUMN)], axis=1)
        g = jnp.concatenate([four[now, r, :, SIDE:] for r in range(PER_COLUMN)], axis=1)
        w_in = jnp.concatenate([w_in_ref[first + r] for r in range(PER_COLUMN)], axis=0)
        w_out = jnp.concatenate([w_out_ref[first + r] for r in range(PER_COLUMN)], axis=1)
        pre_act = jnp.dot(x, w_in, preferred_element_type=jnp.float32)
        activation, gelu_slope = gelu_pair(pre_act)
        grad_act = lax.dot_general(
            g, w_out, (((1,), (1,)), ((), ())), preferred_element_type=jnp.float32
        )
        grad_pre = (grad_act * gelu_slope).astype(jnp.bfloat16)
        over_rows = (((0,), (0,)), ((), ()))
        shares = (
            lax.dot_general(grad_pre, x, over_rows, preferred_element_type=jnp.float32),
            lax.dot_general(
                activation.astype(jnp.bfloat16), g, over_rows, preferred_element_type=jnp.float32
            ),
        )
        for which, share in enumerate(shares):
            for r in range(PER_COLUMN):
                block = share[:, r * SIDE : (r + 1) * SIDE]
                block = (block.T if which == 0 else block).astype(jnp.bfloat16)
                for seq in range(N_SEQ):
                    target = odd if seq % 2 else even
                    target[seq % 8 // 2, seq // 8, which, first + r] = block[
                        seq * 8 : seq * 8 + 8
                    ]


def add_cores(even, odd, seq):
    swap = [(i, i ^ 1) for i in range(N_SEQ)]
    at_odd = seq % 2 == 1
    theirs = lax.ppermute(jnp.where(at_odd, even, odd), "seq", swap)
    mine = jnp.where(at_odd, odd, even)
    return (mine.astype(jnp.float32) + theirs.astype(jnp.float32)).astype(jnp.bfloat16)


def add_along_x(total):
    along_x = [[h * 8 + x * 2 + c for x in range(N_X)] for h in range(2) for c in range(2)]
    total = lax.all_to_all(total, "seq", 0, 0, axis_index_groups=along_x, tiled=True)
    return total.astype(jnp.float32).sum(0)


def add_halves(total, seq):
    across = [(i, i ^ 8) for i in range(N_SEQ)]
    at_high = seq >= N_DEAL
    theirs = jnp.where(at_high, total[0], total[1]).astype(jnp.bfloat16)
    theirs = lax.ppermute(theirs, "seq", across)
    return (jnp.where(at_high, total[1], total[0]) + theirs.astype(jnp.float32)).astype(jnp.bfloat16)


def gather_and_differentiate(size, packed, slots, w_in, w_out):
    vmem = pl.BlockSpec(memory_space=pltpu.VMEM)
    smem = pl.BlockSpec(memory_space=pltpu.SMEM)
    n_slots = w_in.shape[0]
    blocks = {0: packed[:size]}
    passed = []

    def start_along_y(index):
        batch, mask = BATCHES[index]
        value = jnp.stack([blocks[slot] for slot in batch])
        passed.append((value, swap_y(value, mask)))
        return passed[-1][1]

    for i in range(1, 5):
        ahead, behind = blocks[i - 1], blocks[(N_Z - i + 1) % N_Z]
        if i > 2:
            ahead, behind, _ = lax.optimization_barrier((ahead, behind, start_along_y(i - 3)))
        blocks[i] = move_z(ahead, 1)
        if i < 4:
            blocks[N_Z - i] = move_z(behind, -1)
    for index in range(len(passed), len(BATCHES)):
        start_along_y(index)
    passed = [
        part
        for (value, near), (_, mask) in zip(passed, BATCHES)
        for part in (near, swap_y(jnp.concatenate([value, near]), mask ^ 2))
    ]
    any_space = pl.BlockSpec(memory_space=pl.ANY)
    piece = jax.ShapeDtypeStruct((N_X, 2, 2, n_slots, 8, SIDE), jnp.bfloat16)
    return pl.pallas_call(
        grad_kernel,
        out_shape=[piece] * 2,
        in_specs=[smem] + [any_space] * (N_Z + len(passed)) + [vmem] * 2,
        out_specs=[vmem] * 2,
        scratch_shapes=[
            pltpu.VMEM((2, PER_COLUMN, size, 2 * SIDE), jnp.bfloat16),
            pltpu.SemaphoreType.DMA((2, PER_COLUMN)),
        ],
        name="weight_grads",
    )(slots, *[blocks[i] for i in range(N_Z)], *passed, w_in, w_out)


def shards(tokens, grad_out, input_weight_blocks, output_weight_blocks, row_ids, lengths):
    blk, seq = lax.axis_index("blk"), lax.axis_index("seq")
    rows = tokens.shape[0]
    vmem = pl.BlockSpec(memory_space=pltpu.VMEM)
    smem = pl.BlockSpec(memory_space=pltpu.SMEM)
    dealt = pl.pallas_call(
        deal_kernel,
        out_shape=jax.ShapeDtypeStruct((rows + N_DEAL * NOTE_ROWS, 2 * SIDE), jnp.bfloat16),
        in_specs=[smem, smem, vmem, vmem],
        out_specs=vmem,
        name="deal",
    )(lengths, (seq % 2 * (N_DEAL - 1)).reshape(1), tokens, grad_out)
    halves = [[h * N_DEAL + i for i in range(N_DEAL)] for h in range(2)]
    dealt = lax.all_to_all(dealt, "seq", 0, 0, axis_index_groups=halves, tiled=True)
    packed, size = pl.pallas_call(
        pack_kernel,
        out_shape=(
            jax.ShapeDtypeStruct((rows, 2 * SIDE), jnp.bfloat16),
            jax.ShapeDtypeStruct((1,), jnp.int32),
        ),
        in_specs=[vmem],
        out_specs=(vmem, smem),
        name="pack",
    )(dealt)

    place = jnp.array(PLACE, jnp.int32)
    z_slot = (place[blk // N_Y] - place[row_ids // N_Y]) % N_Z
    slots = (z_slot * N_Y + jnp.bitwise_xor(blk, row_ids) % N_Y).astype(jnp.int32)
    slots = jnp.array(whereabouts(), jnp.int32)[slots]
    even, odd = lax.switch(
        size[0],
        [functools.partial(gather_and_differentiate, n) for n in SIZES],
        packed,
        slots,
        input_weight_blocks,
        output_weight_blocks,
    )
    total = add_halves(add_along_x(add_cores(even, odd, seq)), seq)
    return total[0], total[1]


def solution(mesh):
    return jax.shard_map(
        shards,
        mesh=mesh,
        in_specs=(
            P("seq", "blk"),
            P("seq", "blk"),
            P("blk", None, None),
            P("blk", None, None),
            P("blk"),
            P("seq"),
        ),
        out_specs=(P("blk", "seq", None), P("blk", "seq", None)),
        check_vma=False,
    )
```

```python
import functools

import jax
import jax.numpy as jnp
from jax import lax
from jax.experimental import pallas as pl
from jax.experimental.pallas import tpu as pltpu
from jax.sharding import PartitionSpec as P

SIDE = 128
PER_COLUMN = 4
N_SEQ = 16
N_X = 4
N_Y = 4
N_Z = 8
N_DEAL = 8
LIVE = 7680
SIZES = (512, 544, 576, 624, 768)
NOTE_ROWS = 8
DEAD = 256.0
RING = (0, 2, 4, 6, 7, 5, 3, 1)
PLACE = tuple(RING.index(z) for z in range(N_Z))
BATCHES = (((0, 1), 1), ((2, 7), 3), ((3, 4), 1), ((5, 6), 3))

gelu_scale = 0.7978845608


def gelu_pair(pre_act):
    tanh_val = jnp.tanh(gelu_scale * (pre_act + 0.044715 * pre_act * pre_act * pre_act))
    activation = 0.5 * pre_act * (1.0 + tanh_val)
    gelu_slope = 0.5 * (1.0 + tanh_val) + 0.5 * pre_act * (
        1.0 - tanh_val * tanh_val
    ) * gelu_scale * (1.0 + 0.134145 * pre_act * pre_act)
    return (activation, gelu_slope)


def move_z(value, step):
    pairs = [
        (z * N_Y + y, RING[(PLACE[z] + step) % N_Z] * N_Y + y)
        for z in range(N_Z)
        for y in range(N_Y)
    ]
    return lax.ppermute(value, "blk", pairs)


def swap_y(value, mask):
    pairs = [(z * N_Y + y, z * N_Y + (y ^ mask)) for z in range(N_Z) for y in range(N_Y)]
    return lax.ppermute(value, "blk", pairs)


def deal_kernel(length_ref, flip_ref, tokens_ref, grad_ref, out_ref):
    rows = tokens_ref.shape[0]
    out_rows = out_ref.shape[0]
    share, stride = rows // N_DEAL, out_rows // N_DEAL
    at = lax.broadcasted_iota(jnp.int32, (rows, SIDE), 0)
    marked = jnp.where(at < length_ref[0], tokens_ref[...].astype(jnp.float32), DEAD)
    both = jnp.concatenate([marked.astype(jnp.bfloat16), grad_ref[...]], axis=1)
    to = lax.broadcasted_iota(jnp.int32, (out_rows, rows), 0)
    source = lax.broadcasted_iota(jnp.int32, (out_rows, rows), 1)
    slot = jnp.bitwise_xor(source % N_DEAL, flip_ref[0]) * stride + source // N_DEAL
    pick = jnp.where(slot == to, 1.0, 0.0).astype(jnp.bfloat16)
    dealt = jnp.dot(pick, both, preferred_element_type=jnp.float32)
    place = place_in_share(out_rows, 2 * SIDE, stride)
    high = DEAD + 2.0 * (length_ref[0] // 32).astype(jnp.float32)
    low = DEAD + 2.0 * (length_ref[0] % 32).astype(jnp.float32)
    note = jnp.where(place == share, high, jnp.where(place == share + 1, low, DEAD))
    out_ref[...] = jnp.where(place < share, dealt, note).astype(jnp.bfloat16)


def place_in_share(rows, lanes, stride):
    row = lax.broadcasted_iota(jnp.int32, (rows, lanes), 0)
    start = jnp.zeros_like(row)
    for j in range(1, rows // stride):
        start = jnp.where(row >= j * stride, j * stride, start)
    return row - start


def pack_kernel(dealt_ref, out_ref, size_ref):
    rows, out_rows = dealt_ref.shape[0], out_ref.shape[0]
    share = out_rows // N_DEAL
    values = dealt_ref[:, :SIDE].astype(jnp.float32)
    live = jnp.broadcast_to(jnp.where(values[:, :1] < DEAD / 2, 1.0, 0.0), (rows, SIDE))
    place = place_in_share(rows, SIDE, rows // N_DEAL)
    weight = jnp.where(place == share, 16.0, jnp.where(place == share + 1, 0.5, 0.0))
    lane = lax.broadcasted_iota(jnp.int32, (rows, SIDE), 1)
    held = jnp.sum(jnp.where(lane == 0, weight * (values - DEAD), 0.0))
    most = jnp.maximum(held, LIVE - held).astype(jnp.int32) + (N_DEAL - 1) * N_DEAL // 2
    size = jnp.int32(0)
    for smaller in SIZES[:-1]:
        size = size + (most > smaller * N_DEAL).astype(jnp.int32)
    size_ref[0] = size
    stride, ahead, ranks = rows // N_DEAL, jnp.zeros((1, SIDE), jnp.float32), []
    for j in range(N_DEAL):
        here = live[j * stride : (j + 1) * stride]
        at = lax.broadcasted_iota(jnp.int32, (stride, SIDE), 0).astype(jnp.float32)
        ranks.append(jnp.where(here > 0.5, at + ahead, -1.0))
        ahead = ahead + jnp.sum(here, axis=0, keepdims=True)
    rank = jnp.concatenate(ranks, axis=0)[:, :1]
    slot = lax.broadcasted_iota(jnp.int32, (rows, out_rows), 1).astype(jnp.float32)
    pick = jnp.where(rank == slot, 1.0, 0.0).astype(jnp.bfloat16)
    out_ref[...] = lax.dot_general(
        pick, dealt_ref[...], (((0,), (0,)), ((), ())), preferred_element_type=jnp.float32
    ).astype(jnp.bfloat16)


def whereabouts():
    found = [0] * (N_Z * N_Y)
    for slot in range(N_Z):
        found[slot * N_Y] = 4 * slot
    for index, (batch, mask) in enumerate(BATCHES):
        near = 4 * (N_Z + 2 * index)
        for i, slot in enumerate(batch):
            found[slot * N_Y + mask] = near + i
            found[slot * N_Y + (mask ^ 2)] = near + 4 + i
            found[slot * N_Y + 2] = near + 4 + len(batch) + i
    return found


def grad_kernel(where_ref, *refs):
    n_held = N_Z + 2 * len(BATCHES)
    held = refs[:n_held]
    w_in_ref, w_out_ref, even, odd, four, sems = refs[n_held:]
    groups = even.shape[3] // PER_COLUMN

    def fetch(group, into):
        for r in range(PER_COLUMN):
            where = where_ref[group * PER_COLUMN + r]
            for i, ref in enumerate(held):

                def start(ref=ref, r=r, where=where):
                    block = ref if len(ref.shape) == 2 else ref.at[where % 4]
                    pltpu.make_async_copy(block, four.at[into, r], sems.at[into, r]).start()

                pl.when(where // 4 == i)(start)

    fetch(0, 0)

    @pl.loop(0, groups)
    def _(group):
        now = group % 2

        @pl.when(group + 1 < groups)
        def _():
            fetch(group + 1, 1 - now)

        for r in range(PER_COLUMN):
            pltpu.make_async_copy(held[0], four.at[now, r], sems.at[now, r]).wait()
        first = group * PER_COLUMN
        x = jnp.concatenate([four[now, r, :, :SIDE] for r in range(PER_COLUMN)], axis=1)
        g = jnp.concatenate([four[now, r, :, SIDE:] for r in range(PER_COLUMN)], axis=1)
        w_in = jnp.concatenate([w_in_ref[first + r] for r in range(PER_COLUMN)], axis=0)
        w_out = jnp.concatenate([w_out_ref[first + r] for r in range(PER_COLUMN)], axis=1)
        pre_act = jnp.dot(x, w_in, preferred_element_type=jnp.float32)
        activation, gelu_slope = gelu_pair(pre_act)
        grad_act = lax.dot_general(
            g, w_out, (((1,), (1,)), ((), ())), preferred_element_type=jnp.float32
        )
        grad_pre = (grad_act * gelu_slope).astype(jnp.bfloat16)
        over_rows = (((0,), (0,)), ((), ()))
        shares = (
            lax.dot_general(grad_pre, x, over_rows, preferred_element_type=jnp.float32),
            lax.dot_general(
                activation.astype(jnp.bfloat16), g, over_rows, preferred_element_type=jnp.float32
            ),
        )
        for which, share in enumerate(shares):
            for r in range(PER_COLUMN):
                block = share[:, r * SIDE : (r + 1) * SIDE]
                block = block.astype(jnp.bfloat16)
                block = block.T if which == 0 else block
                for seq in range(N_SEQ):
                    target = odd if seq % 2 else even
                    target[seq % 8 // 2, seq // 8, which, first + r] = block[
                        seq * 8 : seq * 8 + 8
                    ]


def add_cores(even, odd, seq):
    swap = [(i, i ^ 1) for i in range(N_SEQ)]
    at_odd = seq % 2 == 1
    theirs = lax.ppermute(jnp.where(at_odd, even, odd), "seq", swap)
    mine = jnp.where(at_odd, odd, even)
    return (mine.astype(jnp.float32) + theirs.astype(jnp.float32)).astype(jnp.bfloat16)


def add_along_x(total):
    along_x = [[h * 8 + x * 2 + c for x in range(N_X)] for h in range(2) for c in range(2)]
    total = lax.all_to_all(total, "seq", 0, 0, axis_index_groups=along_x, tiled=True)
    return total.astype(jnp.float32).sum(0)


def add_halves(total, seq):
    across = [(i, i ^ 8) for i in range(N_SEQ)]
    at_high = seq >= N_DEAL
    theirs = jnp.where(at_high, total[0], total[1]).astype(jnp.bfloat16)
    theirs = lax.ppermute(theirs, "seq", across)
    return (jnp.where(at_high, total[1], total[0]) + theirs.astype(jnp.float32)).astype(jnp.bfloat16)


def gather_and_differentiate(size, packed, slots, w_in, w_out):
    vmem = pl.BlockSpec(memory_space=pltpu.VMEM)
    smem = pl.BlockSpec(memory_space=pltpu.SMEM)
    n_slots = w_in.shape[0]
    blocks = {0: packed[:size]}
    passed = []

    def start_along_y(index):
        batch, mask = BATCHES[index]
        value = jnp.stack([blocks[slot] for slot in batch])
        passed.append((value, swap_y(value, mask)))
        return passed[-1][1]

    for i in range(1, 5):
        ahead, behind = blocks[i - 1], blocks[(N_Z - i + 1) % N_Z]
        if i > 2:
            ahead, behind, _ = lax.optimization_barrier((ahead, behind, start_along_y(i - 3)))
        blocks[i] = move_z(ahead, 1)
        if i < 4:
            blocks[N_Z - i] = move_z(behind, -1)
    for index in range(len(passed), len(BATCHES)):
        start_along_y(index)
    passed = [
        part
        for (value, near), (_, mask) in zip(passed, BATCHES)
        for part in (near, swap_y(jnp.concatenate([value, near]), mask ^ 2))
    ]
    any_space = pl.BlockSpec(memory_space=pl.ANY)
    piece = jax.ShapeDtypeStruct((N_X, 2, 2, n_slots, 8, SIDE), jnp.bfloat16)
    return pl.pallas_call(
        grad_kernel,
        out_shape=[piece] * 2,
        in_specs=[smem] + [any_space] * (N_Z + len(passed)) + [vmem] * 2,
        out_specs=[vmem] * 2,
        scratch_shapes=[
            pltpu.VMEM((2, PER_COLUMN, size, 2 * SIDE), jnp.bfloat16),
            pltpu.SemaphoreType.DMA((2, PER_COLUMN)),
        ],
        name="weight_grads",
    )(slots, *[blocks[i] for i in range(N_Z)], *passed, w_in, w_out)


def shards(tokens, grad_out, input_weight_blocks, output_weight_blocks, row_ids, lengths):
    blk, seq = lax.axis_index("blk"), lax.axis_index("seq")
    rows = tokens.shape[0]
    vmem = pl.BlockSpec(memory_space=pltpu.VMEM)
    smem = pl.BlockSpec(memory_space=pltpu.SMEM)
    dealt = pl.pallas_call(
        deal_kernel,
        out_shape=jax.ShapeDtypeStruct((rows + N_DEAL * NOTE_ROWS, 2 * SIDE), jnp.bfloat16),
        in_specs=[smem, smem, vmem, vmem],
        out_specs=vmem,
        name="deal",
    )(lengths, (seq % 2 * (N_DEAL - 1)).reshape(1), tokens, grad_out)
    halves = [[h * N_DEAL + i for i in range(N_DEAL)] for h in range(2)]
    dealt = lax.all_to_all(dealt, "seq", 0, 0, axis_index_groups=halves, tiled=True)
    packed, size = pl.pallas_call(
        pack_kernel,
        out_shape=(
            jax.ShapeDtypeStruct((rows, 2 * SIDE), jnp.bfloat16),
            jax.ShapeDtypeStruct((1,), jnp.int32),
        ),
        in_specs=[vmem],
        out_specs=(vmem, smem),
        name="pack",
    )(dealt)

    place = jnp.array(PLACE, jnp.int32)
    z_slot = (place[blk // N_Y] - place[row_ids // N_Y]) % N_Z
    slots = (z_slot * N_Y + jnp.bitwise_xor(blk, row_ids) % N_Y).astype(jnp.int32)
    slots = jnp.array(whereabouts(), jnp.int32)[slots]
    even, odd = lax.switch(
        size[0],
        [functools.partial(gather_and_differentiate, n) for n in SIZES],
        packed,
        slots,
        input_weight_blocks,
        output_weight_blocks,
    )
    total = add_halves(add_along_x(add_cores(even, odd, seq)), seq)
    return total[0], total[1]


def solution(mesh):
    return jax.shard_map(
        shards,
        mesh=mesh,
        in_specs=(
            P("seq", "blk"),
            P("seq", "blk"),
            P("blk", None, None),
            P("blk", None, None),
            P("blk"),
            P("seq"),
        ),
        out_specs=(P("blk", "seq", None), P("blk", "seq", None)),
        check_vma=False,
    )
```
